256 devices in a mesh: frame: 32 (over y, z), space: 8 (over x, core).
Axes of the slice: x: 4, y: 4, z: 8, core: 2. Of those that a mesh axis runs over, the one named last changes fastest.
Arguments:
- queries: float32 [32, 2048, 1120], P('frame', 'space'), may hold values from -6 to 6
- keys: float32 [32, 2048, 1120], P('frame', 'space'), may hold values from -6 to 6
- values: float32 [32, 2048, 1120], P('frame', 'space'), may hold values from -6 to 6
- cotangent: float32 [32, 2048, 1120], P('frame', 'space'), may hold values from -6 to 6
Outputs:
- query_grad: float32 [32, 2048, 1120], P('frame', 'space')
- key_grad: float32 [32, 2048, 1120], P('frame', 'space')
- value_grad: float32 [32, 2048, 1120], P('frame', 'space')
The draws below stay inside these ranges and needn't reach their ends.
All inputs are finite; a program needn't handle non-finite values.
Results may differ from the reference program's by a relative error of at most 0.0003.
Values sent between devices are 32-bit elements; how exact they have to be, the bound alone decides.
No kernel may reach another device: no remote copies, remote signals or barrier semaphores. Data moves between devices by JAX's collectives and lax.ppermute only.
A program may use at most 64 MiB of HBM per device.

```python
import jax
import jax.numpy as jnp
from jax import lax

HEAD = 112
D = 1120
FRAMES = 32
SPATIAL = 2048


def draw_field(key, salt):
    base = jax.random.fold_in(key, salt)
    entry_key = jax.random.fold_in(base, 0)
    field = jax.random.normal(entry_key, (FRAMES, SPATIAL, D), jnp.float32)
    return jnp.clip(field, -6.0, 6.0)


def draw_queries(key, part):
    return draw_field(key, 101)


def draw_keys(key, part):
    return draw_field(key, 202)


def draw_values(key, part):
    return draw_field(key, 303)


def draw_cotangent(key, part):
    return draw_field(key, 404)


def setup_inputs(seed: int = 0) -> dict:
    seeds = jax.random.split(jax.random.key(seed), 5)
    queries = draw_queries(jax.random.fold_in(seeds[4], 71), 0)
    keys = draw_keys(jax.random.fold_in(seeds[4], 71), 0)
    values = draw_values(jax.random.fold_in(seeds[4], 71), 0)
    cotangent = draw_cotangent(jax.random.fold_in(seeds[4], 71), 0)
    return {"queries": queries, "keys": keys, "values": values, "cotangent": cotangent}


def outer_states(left, right):
    frames, spatial, model_width = left.shape
    head_count = model_width // HEAD
    left_heads = left.reshape(frames, spatial, head_count, HEAD)
    right_heads = right.reshape(frames, spatial, head_count, HEAD)
    result = jnp.einsum('fshi,fshj->fihj', left_heads, right_heads, precision=lax.Precision.HIGHEST)
    return result.reshape(frames, HEAD, model_width)

def reference(queries, keys, values, cotangent):
    frames, spatial, model_width = queries.shape
    head_count = model_width // HEAD
    counts = (jnp.arange(frames, dtype=jnp.int32) + 1).astype(jnp.float32) * (spatial * HEAD)
    scales = 1.0 / jnp.sqrt(counts)
    pos_q = jnp.maximum(queries, 0.0)
    pos_k = jnp.maximum(keys, 0.0)
    kv_block = outer_states(pos_k, values)
    qd_block = outer_states(pos_q, cotangent) * scales[:, None, None]
    state = jnp.cumsum(kv_block, axis=0).reshape(frames, HEAD, head_count, HEAD)
    grad_state = jnp.flip(jnp.cumsum(jnp.flip(qd_block, 0), axis=0), 0).reshape(frames, HEAD, head_count, HEAD)
    cot_heads = cotangent.reshape(frames, spatial, head_count, HEAD)
    val_heads = values.reshape(frames, spatial, head_count, HEAD)
    posk_heads = pos_k.reshape(frames, spatial, head_count, HEAD)
    hp = lax.Precision.HIGHEST
    query_grad = jnp.einsum('fshj,fihj->fshi', cot_heads, state, precision=hp).reshape(frames, spatial, model_width)
    query_grad = jnp.where(queries > 0, query_grad * scales[:, None, None], 0.0)
    key_grad = jnp.einsum('fshj,fihj->fshi', val_heads, grad_state, precision=hp).reshape(frames, spatial, model_width)
    key_grad = jnp.where(keys > 0, key_grad, 0.0)
    value_grad = jnp.einsum('fshi,fihj->fshj', posk_heads, grad_state, precision=hp).reshape(frames, spatial, model_width)
    return (query_grad, key_grad, value_grad)
```

```python
import functools

import jax
import jax.numpy as jnp
from jax import lax
from jax.experimental import pallas as pl
from jax.experimental.pallas import tpu as pltpu
from jax.sharding import Mesh
from jax.sharding import PartitionSpec as P

HEAD = 112
LANES = 128
ROWS = HEAD // 8


def head_span(lo, hi):
    return lo // HEAD, (hi - 1) // HEAD


def split(x):
    hi = x.astype(jnp.bfloat16)
    return hi, (x - hi.astype(jnp.float32)).astype(jnp.bfloat16)


def dot3(a, b, dims):
    (ah, al), (bh, bl) = a, b
    d = functools.partial(lax.dot_general, dimension_numbers=(dims, ((), ())), preferred_element_type=jnp.float32)
    return d(ah, bh) + (d(ah, bl) + d(al, bh))


def gram_kernel(first, width, sel_ref, scale_ref, q_ref, k_ref, v_ref, c_ref, out_ref, left, right, sems):
    use_q = sel_ref[0] == first

    @pl.when(use_q)
    def _():
        pltpu.make_async_copy(q_ref.at[0], left, sems.at[0]).start()
        pltpu.make_async_copy(c_ref.at[0], right, sems.at[1]).start()

    @pl.when(jnp.logical_not(use_q))
    def _():
        pltpu.make_async_copy(k_ref.at[0], left, sems.at[0]).start()
        pltpu.make_async_copy(v_ref.at[0], right, sems.at[1]).start()

    scale = jnp.where(use_q, scale_ref[0], 1.0)
    pltpu.make_async_copy(k_ref.at[0], left, sems.at[0]).wait()
    pltpu.make_async_copy(v_ref.at[0], right, sems.at[1]).wait()
    for g in range(0, width, 2 * LANES):
        end = min(g + 2 * LANES, width)
        h0, h1 = head_span(g, end)
        r = split(right[:, g:end])
        lo = h0 * HEAD // LANES * LANES
        hi = min(-(-(h1 + 1) * HEAD // LANES) * LANES, width)
        lt = split(jnp.maximum(left[:, lo:hi], 0.0).T)
        base = h0 * HEAD - lo
        n = (h1 - h0 + 1) * HEAD
        gram = dot3([t[base : base + n] for t in lt], r, ((1,), (0,))) * scale
        for l in range(g // LANES, -(-end // LANES)):
            cols = min((l + 1) * LANES, width) - l * LANES
            a, b = head_span(l * LANES, l * LANES + cols)
            block = [gram[(h - h0) * HEAD : (h - h0 + 1) * HEAD, l * LANES - g : l * LANES - g + cols] for h in range(a, b + 1)]
            tile = block[0]
            if b > a:
                lane = lax.broadcasted_iota(jnp.int32, tile.shape, 1)
                tile = jnp.where(lane < b * HEAD - l * LANES, block[0], block[1])
            if cols < LANES:
                tile = jnp.concatenate([tile, jnp.zeros((HEAD, LANES - cols), jnp.float32)], axis=1)
            out_ref[l * ROWS : (l + 1) * ROWS] = tile.reshape(ROWS, 8, LANES)
    used = -(-width // LANES) * ROWS
    if used < out_ref.shape[0]:
        out_ref[used:] = jnp.zeros((out_ref.shape[0] - used, 8, LANES), jnp.float32)


def gram_state(first, sel, scale, q, k, v, cot, tiles):
    spatial, width = q.shape[1:]
    smem = pl.BlockSpec(memory_space=pltpu.SMEM)
    hbm = pl.BlockSpec(memory_space=pl.ANY)
    return pl.pallas_call(
        functools.partial(gram_kernel, first, width),
        out_shape=jax.ShapeDtypeStruct((tiles, 8, LANES), jnp.float32),
        in_specs=[smem, smem, hbm, hbm, hbm, hbm],
        out_specs=pl.BlockSpec(memory_space=pltpu.VMEM),
        scratch_shapes=[
            pltpu.VMEM((spatial, width), jnp.float32),
            pltpu.VMEM((spatial, width), jnp.float32),
            pltpu.SemaphoreType.DMA((2,)),
        ],
        cost_estimate=pl.CostEstimate(flops=2 * 3 * spatial * HEAD * width, bytes_accessed=8 * spatial * width, transcendentals=0),
        name="gram",
    )(sel, scale, q, k, v, cot)


def fill_band(width, st_ref, wh, wl):
    for l in range(-(-width // LANES)):
        cols = min((l + 1) * LANES, width) - l * LANES
        a, b = head_span(l * LANES, l * LANES + cols)
        s = st_ref[l * ROWS : (l + 1) * ROWS].reshape(HEAD, LANES)
        lane = lax.broadcasted_iota(jnp.int32, s.shape, 1) + l * LANES
        for h in range(a, b + 1):
            hi, lo = split(jnp.where((lane >= h * HEAD) & (lane < (h + 1) * HEAD), s, 0.0))
            wh[h * HEAD : (h + 1) * HEAD, l * LANES : (l + 1) * LANES] = hi
            wl[h * HEAD : (h + 1) * HEAD, l * LANES : (l + 1) * LANES] = lo


def groups(width):
    for g in range(0, width, 2 * LANES):
        end = min(g + 2 * LANES, width)
        h0, h1 = head_span(g, end)
        yield g, end, h0 * HEAD // LANES * LANES, min(-(-(h1 + 1) * HEAD // LANES) * LANES, width)


def grads_kernel(width, xs_ref, scale_ref, q_ref, k_ref, v_ref, c_ref, *rest):
    own, other, outs, (qb, kb, vb, cb, st, wh, wl, og, sems, osems) = rest[:4], rest[4:8], rest[8:11], rest[11:]
    loads = [
        pltpu.make_async_copy(src.at[0], dst, sems.at[i])
        for i, (src, dst) in enumerate(((q_ref, qb), (k_ref, kb), (v_ref, vb), (c_ref, cb)))
    ]
    for load in loads:
        load.start()
    x, core = xs_ref[0], xs_ref[1]
    n = own[0].shape[0]
    for i, (a, b) in enumerate(zip(own, other)):
        piece = lax.rem(x + 4 - i, 4)
        st[core, pl.ds(piece * n, n)] = a[...]
        st[1 - core, pl.ds(piece * n, n)] = b[...]
    wh[...] = jnp.zeros_like(wh)
    wl[...] = jnp.zeros_like(wl)
    for load in loads:
        load.wait()
    scale = scale_ref[0]
    fill_band(width, st.at[0], wh, wl)
    for g, end, lo, hi in groups(width):
        w = wh[g:end, lo:hi], wl[g:end, lo:hi]
        out = dot3(split(cb[:, lo:hi]), w, ((1,), (1,)))
        og[0, :, g:end] = jnp.where(qb[:, g:end] > 0, out * scale, 0.0)
    stores = [pltpu.make_async_copy(og.at[i], outs[i].at[0], osems.at[i]) for i in range(3)]
    stores[0].start()
    fill_band(width, st.at[1], wh, wl)
    for g, end, lo, hi in groups(width):
        w = wh[g:end, lo:hi], wl[g:end, lo:hi]
        out = dot3(split(vb[:, lo:hi]), w, ((1,), (1,)))
        og[1, :, g:end] = jnp.where(kb[:, g:end] > 0, out, 0.0)
    stores[1].start()
    for g, end, lo, hi in groups(width):
        w = wh[lo:hi, g:end], wl[lo:hi, g:end]
        og[2, :, g:end] = dot3(split(jnp.maximum(kb[:, lo:hi], 0.0)), w, ((1,), (0,)))
    stores[2].start()
    for store in stores:
        store.wait()


def gradients(xs, scale, q, k, v, cot, own, other):
    _, spatial, width = q.shape
    tiles = 4 * own[0].shape[0]
    padded = -(-width // LANES) * LANES
    smem = pl.BlockSpec(memory_space=pltpu.SMEM)
    hbm = pl.BlockSpec(memory_space=pl.ANY)
    vmem = pl.BlockSpec(memory_space=pltpu.VMEM)
    array = pltpu.VMEM((spatial, width), jnp.float32)
    return pl.pallas_call(
        functools.partial(grads_kernel, width),
        out_shape=[jax.ShapeDtypeStruct(q.shape, jnp.float32)] * 3,
        in_specs=[smem, smem, hbm, hbm, hbm, hbm] + [vmem] * 8,
        out_specs=[hbm] * 3,
        scratch_shapes=[
            array,
            array,
            array,
            array,
            pltpu.VMEM((2, tiles, 8, LANES), jnp.float32),
            pltpu.VMEM((width, padded), jnp.bfloat16),
            pltpu.VMEM((width, padded), jnp.bfloat16),
            pltpu.VMEM((3, spatial, width), jnp.float32),
            pltpu.SemaphoreType.DMA((4,)),
            pltpu.SemaphoreType.DMA((3,)),
        ],
        name="grads",
    )(xs, scale, q, k, v, cot, *own, *other)


def ring(n, k):
    return [(i, (i + k) % n) for i in range(n)]


def shards(queries, keys, values, cotangent):
    _, spatial, width = queries.shape
    ny, nz, nx, nc = (lax.axis_size(a) for a in ("y", "z", "x", "c"))
    y, z, x, c = (lax.axis_index(a) for a in ("y", "z", "x", "c"))
    count = (y * nz + z + 1).astype(jnp.float32) * (spatial * nx * nc * HEAD)
    scale = (1.0 / jnp.sqrt(count)).reshape(1)
    sel = c.astype(jnp.int32).reshape(1)
    step = nx * nz
    tiles = -(-(ROWS * -(-width // LANES)) // step) * step

    args = (sel, scale, queries, keys, values, cotangent, tiles)
    sent = gram_state(0, *args)
    got = lax.ppermute(sent, "c", ring(nc, 1))
    both = gram_state(1, *args) + got

    n = tiles // nx
    piece = lambda k: lax.dynamic_slice_in_dim(both, lax.rem(x + k, nx) * n, n, 0)
    mine = piece(0)
    arrived = [lax.ppermute(piece(k), "x", ring(nx, k)) for k in (1, 3, 2)]
    mine = (mine + arrived[0]) + (arrived[1] + arrived[2])

    g = mine.reshape(nz, n // nz, 8, LANES)
    g = lax.all_to_all(g, "z", split_axis=0, concat_axis=0, tiled=True)
    total = g.sum(axis=0)
    carry = 0.0
    for k in range(1, ny):
        pairs = [(i * nc, (i + k) * nc) for i in range(ny - k)] + [((i + k) * nc + 1, i * nc + 1) for i in range(ny - k)]
        carry = carry + lax.ppermute(total, ("y", "c"), pairs)
    up, down = [], []
    run_up = run_down = carry
    for j in range(nz):
        run_up = run_up + g[j]
        up.append(run_up)
        run_down = run_down + g[nz - 1 - j]
        down.append(run_down)
    scanned = jnp.where(c == 0, jnp.stack(up), jnp.stack(down[::-1]))
    mine = lax.all_to_all(scanned, "z", split_axis=0, concat_axis=0, tiled=True)
    mine = mine.reshape(n, 8, LANES)

    own = [mine] + [lax.ppermute(mine, "x", ring(nx, k)) for k in range(1, nx)]
    other = [lax.ppermute(p, "c", ring(nc, 1)) for p in own]
    xs = jnp.stack([x, c]).astype(jnp.int32)
    return gradients(xs, scale, queries, keys, values, cotangent, own, other)


def solution(mesh):
    torus = Mesh(mesh.devices.reshape(4, 8, 4, 2), ("y", "z", "x", "c"))
    spec = P(("y", "z"), ("x", "c"), None)
    return jax.shard_map(shards, mesh=torus, in_specs=(spec,) * 4, out_specs=(spec,) * 3, check_vma=False)
```

```python
import functools

import jax
import jax.numpy as jnp
from jax import lax
from jax.experimental import pallas as pl
from jax.experimental.pallas import tpu as pltpu
from jax.sharding import Mesh
from jax.sharding import PartitionSpec as P

HEAD = 112
LANES = 128
ROWS = HEAD // 8


def split(x):
    hi = x.astype(jnp.bfloat16)
    return hi, (x - hi.astype(jnp.float32)).astype(jnp.bfloat16)


def dot3(a, b, dims):
    (ah, al), (bh, bl) = a, b
    d = functools.partial(lax.dot_general, dimension_numbers=(dims, ((), ())), preferred_element_type=jnp.float32)
    return d(ah, bh) + (d(ah, bl) + d(al, bh))


SPLIT = 7
SPARE = LANES - HEAD


def gram_kernel(first, heads, scale_ref, q_ref, k_ref, v_ref, c_ref, out_ref, left, right, sems):
    use_q = lax.axis_index("c") == first
    order = [SPLIT] + [h for h in range(heads) if h != SPLIT]

    def rows(h):
        return pl.ds(h * HEAD, HEAD)

    def copies(l_ref, r_ref, h):
        return (
            pltpu.make_async_copy(l_ref.at[0, rows(h)], left.at[rows(h)], sems.at[0, h]),
            pltpu.make_async_copy(r_ref.at[0, rows(h)], right.at[rows(h)], sems.at[1, h]),
        )

    @pl.when(use_q)
    def _():
        for h in order:
            for copy in copies(q_ref, c_ref, h):
                copy.start()

    @pl.when(jnp.logical_not(use_q))
    def _():
        for h in order:
            for copy in copies(k_ref, v_ref, h):
                copy.start()

    scale = jnp.where(use_q, scale_ref[0], 1.0)

    def state(l, r):
        return dot3(l, r, ((1,), (1,))) * scale

    for h in order:
        for copy in copies(k_ref, v_ref, h):
            copy.wait()
        lh = split(jnp.maximum(left[rows(h)], 0.0))
        rh = split(right[rows(h)])
        if h == SPLIT:
            l7, r7 = lh, rh
            continue
        if h < SPLIT:
            part = slice(h * SPARE, (h + 1) * SPARE)
            lh = [jnp.concatenate([a, b], axis=0) for a, b in zip(lh, l7)]
            rh = [jnp.concatenate([a, b[part]], axis=0) for a, b in zip(rh, r7)]
            gram = state(lh, rh)
            lane = lax.broadcasted_iota(jnp.int32, (HEAD, LANES), 1)
            block, at = jnp.where(lane < HEAD, gram[:HEAD], gram[HEAD:]), h
        else:
            block, at = state(lh, rh), h - 1
            block = jnp.concatenate([block, jnp.zeros((HEAD, SPARE), jnp.float32)], axis=1)
        out_ref[at * ROWS : (at + 1) * ROWS] = block.reshape(ROWS, 8, LANES)
    used = (heads - 1) * ROWS
    out_ref[used:] = jnp.zeros((out_ref.shape[0] - used, 8, LANES), jnp.float32)


def gram_state(first, scale, q, k, v, cot, tiles):
    width, spatial = q.shape[1:]
    heads = width // HEAD
    smem = pl.BlockSpec(memory_space=pltpu.SMEM)
    hbm = pl.BlockSpec(memory_space=pltpu.HBM)
    return pl.pallas_call(
        functools.partial(gram_kernel, first, heads),
        out_shape=jax.ShapeDtypeStruct((tiles, 8, LANES), jnp.float32),
        in_specs=[smem, hbm, hbm, hbm, hbm],
        out_specs=pl.BlockSpec(memory_space=pltpu.VMEM),
        scratch_shapes=[
            pltpu.VMEM((width, spatial), jnp.float32),
            pltpu.VMEM((width, spatial), jnp.float32),
            pltpu.SemaphoreType.DMA((2, heads)),
        ],
        compiler_params=pltpu.CompilerParams(vmem_limit_bytes=65_000_000),
        cost_estimate=pl.CostEstimate(flops=2 * 3 * spatial * HEAD * width, bytes_accessed=8 * spatial * width, transcendentals=0),
        name="gram",
    )(scale, q, k, v, cot)


def grads_kernel(heads, scale_ref, q_ref, k_ref, v_ref, c_ref, *rest):
    own, other, outs, (qb, kb, vb, cb, st, og, sems, psems, osems) = rest[:4], rest[4:8], rest[8:11], rest[11:]

    def rows(h):
        return pl.ds(h * HEAD, HEAD)

    x, core = lax.axis_index("x"), lax.axis_index("c")
    n = own[0].shape[0]
    states = []
    for i, (a, b) in enumerate(zip(own, other)):
        at = pl.ds(lax.rem(x + 4 - i, 4) * n, n)
        states.append(pltpu.make_async_copy(a, st.at[core, at], psems.at[0, i]))
        states.append(pltpu.make_async_copy(b, st.at[1 - core, at], psems.at[1, i]))
    for copy in states:
        copy.start()
    loads = {
        (i, h): pltpu.make_async_copy(src.at[0, rows(h)], dst.at[rows(h)], sems.at[i, h])
        for pair in ((0, 1), (2, 3))
        for h in range(heads)
        for i, (src, dst) in enumerate(((c_ref, cb), (q_ref, qb), (v_ref, vb), (k_ref, kb)))
        if i in pair
    }
    for load in loads.values():
        load.start()
    scale = scale_ref[0]
    for copy in states:
        copy.wait()

    def state(kind, h):
        def block(at):
            return st[kind, at * ROWS : (at + 1) * ROWS].reshape(HEAD, LANES)

        if h == SPLIT:
            return jnp.concatenate([block(i)[:, HEAD:] for i in range(SPLIT)], axis=1)
        return block(h if h < SPLIT else h - 1)[:, :HEAD]

    nn = ((1,), (0,))
    stores = []

    def store(i, h):
        copy = pltpu.make_async_copy(og.at[i, rows(h)], outs[i].at[0, rows(h)], osems.at[i, h])
        copy.start()
        stores.append(copy)

    for h in range(heads):
        loads[0, h].wait()
        loads[1, h].wait()
        out = dot3(split(state(0, h) * scale), split(cb[rows(h)]), nn)
        og[0, rows(h)] = jnp.where(qb[rows(h)] > 0, out, 0.0)
        store(0, h)
    for h in range(heads):
        loads[2, h].wait()
        loads[3, h].wait()
        s = state(1, h)
        out = dot3(split(s), split(vb[rows(h)]), nn)
        og[1, rows(h)] = jnp.where(kb[rows(h)] > 0, out, 0.0)
        store(1, h)
        og[2, rows(h)] = dot3(split(s.T), split(jnp.maximum(kb[rows(h)], 0.0)), nn)
        store(2, h)
    for copy in stores:
        copy.wait()


def gradients(scale, q, k, v, cot, own, other):
    _, width, spatial = q.shape
    heads = width // HEAD
    tiles = 4 * own[0].shape[0]
    smem = pl.BlockSpec(memory_space=pltpu.SMEM)
    hbm = pl.BlockSpec(memory_space=pl.ANY)
    array = pltpu.VMEM((width, spatial), jnp.float32)
    return pl.pallas_call(
        functools.partial(grads_kernel, heads),
        out_shape=[jax.ShapeDtypeStruct(q.shape, jnp.float32)] * 3,
        in_specs=[smem, hbm, hbm, hbm, hbm] + [hbm] * 8,
        out_specs=[hbm] * 3,
        scratch_shapes=[
            array,
            array,
            array,
            array,
            pltpu.VMEM((2, tiles, 8, LANES), jnp.float32),
            pltpu.VMEM((3, width, spatial), jnp.float32),
            pltpu.SemaphoreType.DMA((4, heads)),
            pltpu.SemaphoreType.DMA((2, 4)),
            pltpu.SemaphoreType.DMA((3, heads)),
        ],
        compiler_params=pltpu.CompilerParams(vmem_limit_bytes=16 << 20),
        name="grads",
    )(scale, q, k, v, cot, *own, *other)


def ring(n, k):
    return [(i, (i + k) % n) for i in range(n)]


def shards(queries, keys, values, cotangent):
    queries, keys, values, cotangent = (jnp.swapaxes(a, 1, 2) for a in (queries, keys, values, cotangent))
    _, width, spatial = queries.shape
    ny, nz, nx, nc = (lax.axis_size(a) for a in ("y", "z", "x", "c"))
    y, z, x, c = (lax.axis_index(a) for a in ("y", "z", "x", "c"))
    count = (y * nz + z + 1).astype(jnp.float32) * (spatial * nx * nc * HEAD)
    scale = (1.0 / jnp.sqrt(count)).reshape(1)
    step = nx * nz
    tiles = -(-(ROWS * (width // HEAD - 1)) // step) * step

    args = (scale, queries, keys, values, cotangent, tiles)
    sent = gram_state(0, *args)
    got = lax.ppermute(sent, "c", ring(nc, 1))
    both = gram_state(1, *args) + got

    n = tiles // nx
    piece = lambda k: lax.dynamic_slice_in_dim(both, lax.rem(x + k, nx) * n, n, 0)
    mine = piece(0)
    arrived = [lax.ppermute(piece(k), "x", ring(nx, k)) for k in (1, 3, 2)]
    mine = (mine + arrived[0]) + (arrived[1] + arrived[2])

    g = mine.reshape(nz, n // nz, 8, LANES)
    g = lax.all_to_all(g, "z", split_axis=0, concat_axis=0, tiled=True)
    total = g.sum(axis=0)
    carry = 0.0
    for k in range(1, ny):
        pairs = [(i * nc, (i + k) * nc) for i in range(ny - k)] + [((i + k) * nc + 1, i * nc + 1) for i in range(ny - k)]
        carry = carry + lax.ppermute(total, ("y", "c"), pairs)
    up, down = [], []
    run_up = run_down = carry
    for j in range(nz):
        run_up = run_up + g[j]
        up.append(run_up)
        run_down = run_down + g[nz - 1 - j]
        down.append(run_down)
    scanned = jnp.where(c == 0, jnp.stack(up), jnp.stack(down[::-1]))
    mine = lax.all_to_all(scanned, "z", split_axis=0, concat_axis=0, tiled=True)
    mine = mine.reshape(n, 8, LANES)

    own = [mine] + [lax.ppermute(mine, "x", ring(nx, k)) for k in range(1, nx)]
    other = [lax.ppermute(p, "c", ring(nc, 1)) for p in own]
    grads = gradients(scale, queries, keys, values, cotangent, own, other)
    return tuple(jnp.swapaxes(a, 1, 2) for a in grads)


def solution(mesh):
    torus = Mesh(mesh.devices.reshape(4, 8, 4, 2), ("y", "z", "x", "c"))
    spec = P(("y", "z"), ("x", "c"), None)
    return jax.shard_map(shards, mesh=torus, in_specs=(spec,) * 4, out_specs=(spec,) * 3, check_vma=False)
```

```python
import functools

import jax
import jax.numpy as jnp
from jax import lax
from jax.experimental import pallas as pl
from jax.experimental.pallas import tpu as pltpu
from jax.sharding import Mesh
from jax.sharding import PartitionSpec as P

HEAD = 112
LANES = 128
ROWS = HEAD // 8


def split(x):
    hi = x.astype(jnp.bfloat16)
    return hi, (x - hi.astype(jnp.float32)).astype(jnp.bfloat16)


def dot3(a, b, dims):
    (ah, al), (bh, bl) = a, b
    d = functools.partial(lax.dot_general, dimension_numbers=(dims, ((), ())), preferred_element_type=jnp.float32)
    return d(ah, bh) + (d(ah, bl) + d(al, bh))


SPLIT = 7
SPARE = LANES - HEAD
PAIR = 2 * LANES


def head_rows(h):
    return pl.ds(h * HEAD, HEAD)


def slot_rows(h):
    return pl.ds(h * LANES, HEAD)


def clear_pads(heads, *refs):
    for ref in refs:
        for h in range(heads):
            ref[h * LANES + HEAD : (h + 1) * LANES] = jnp.zeros((SPARE, ref.shape[1]), jnp.float32)


def lane_of(shape):
    return lax.broadcasted_iota(jnp.int32, shape, 1)


def gram_kernel(first, heads, scale_ref, q_ref, k_ref, v_ref, c_ref, out_ref, left, right, sems):
    use_q = lax.axis_index("c") == first
    order = [SPLIT // 2] + [p for p in range(heads // 2) if p != SPLIT // 2]

    def copies(l_ref, r_ref, h):
        return (
            pltpu.make_async_copy(l_ref.at[0, head_rows(h)], left.at[slot_rows(h)], sems.at[0, h]),
            pltpu.make_async_copy(r_ref.at[0, head_rows(h)], right.at[slot_rows(h)], sems.at[1, h]),
        )

    def start(l_ref, r_ref):
        for p in order:
            for h in (2 * p, 2 * p + 1):
                for copy in copies(l_ref, r_ref, h):
                    copy.start()

    @pl.when(use_q)
    def _():
        start(q_ref, c_ref)

    @pl.when(jnp.logical_not(use_q))
    def _():
        start(k_ref, v_ref)

    clear_pads(heads, left, right)
    scale = jnp.where(use_q, scale_ref[0], 1.0)
    for p in order:
        for h in (2 * p, 2 * p + 1):
            for copy in copies(k_ref, v_ref, h):
                copy.wait()
        l = split(jnp.maximum(left[p * PAIR : (p + 1) * PAIR], 0.0))
        r = split(right[p * PAIR : (p + 1) * PAIR])
        gram = dot3(l, r, ((1,), (1,))) * scale
        blocks = gram[:HEAD, :LANES], gram[LANES : LANES + HEAD, LANES:]
        if p == SPLIT // 2:
            shared = blocks[SPLIT % 2]
        for h, block in zip((2 * p, 2 * p + 1), blocks):
            if h == SPLIT:
                continue
            if h < SPLIT:
                part = pltpu.roll(shared, HEAD - h * SPARE, 1) if h * SPARE < HEAD else shared
                block = jnp.where(lane_of(block.shape) < HEAD, block, part)
            at = h if h < SPLIT else h - 1
            out_ref[at * ROWS : (at + 1) * ROWS] = block.reshape(ROWS, 8, LANES)
    used = (heads - 1) * ROWS
    out_ref[used:] = jnp.zeros((out_ref.shape[0] - used, 8, LANES), jnp.float32)


def gram_state(first, scale, q, k, v, cot, tiles):
    width, spatial = q.shape[1:]
    heads = width // HEAD
    smem = pl.BlockSpec(memory_space=pltpu.SMEM)
    hbm = pl.BlockSpec(memory_space=pl.ANY)
    return pl.pallas_call(
        functools.partial(gram_kernel, first, heads),
        out_shape=jax.ShapeDtypeStruct((tiles, 8, LANES), jnp.float32),
        in_specs=[smem, hbm, hbm, hbm, hbm],
        out_specs=pl.BlockSpec(memory_space=pltpu.VMEM),
        scratch_shapes=[
            pltpu.VMEM((heads * LANES, spatial), jnp.float32),
            pltpu.VMEM((heads * LANES, spatial), jnp.float32),
            pltpu.SemaphoreType.DMA((2, heads)),
        ],
        compiler_params=pltpu.CompilerParams(vmem_limit_bytes=16 << 20),
        cost_estimate=pl.CostEstimate(flops=2 * 3 * spatial * HEAD * width, bytes_accessed=8 * spatial * width, transcendentals=0),
        name="gram",
    )(scale, q, k, v, cot)


def grads_kernel(heads, scale_ref, q_ref, k_ref, v_ref, c_ref, *rest):
    own, other, outs, (qb, kb, vb, cb, st, og, sems, psems, osems) = rest[:4], rest[4:8], rest[8:11], rest[11:]
    x, core = lax.axis_index("x"), lax.axis_index("c")
    n = own[0].shape[0]
    states = []
    for i, (a, b) in enumerate(zip(own, other)):
        at = pl.ds(lax.rem(x + 4 - i, 4) * n, n)
        states.append(pltpu.make_async_copy(a, st.at[core, at], psems.at[0, i]))
        states.append(pltpu.make_async_copy(b, st.at[1 - core, at], psems.at[1, i]))
    for copy in states:
        copy.start()
    loads = {
        (i, h): pltpu.make_async_copy(src.at[0, head_rows(h)], dst.at[slot_rows(h)], sems.at[i, h])
        for pair in ((0, 1), (2, 3))
        for h in range(heads)
        for i, (src, dst) in enumerate(((c_ref, cb), (q_ref, qb), (v_ref, vb), (k_ref, kb)))
        if i in pair
    }
    for load in loads.values():
        load.start()
    clear_pads(heads, cb, vb, kb)
    scale = scale_ref[0]
    for copy in states:
        copy.wait()

    def state(kind, h):
        def block(at):
            return st[kind, at * ROWS : (at + 1) * ROWS].reshape(HEAD, LANES)

        if h == SPLIT:
            s = jnp.zeros((HEAD, LANES), jnp.float32)
            for i in range(SPLIT):
                lane = lane_of(s.shape)
                part = pltpu.roll(block(i), (i + 1) * SPARE, 1)
                s = jnp.where((lane >= i * SPARE) & (lane < (i + 1) * SPARE), part, s)
        else:
            s = block(h if h < SPLIT else h - 1)
            s = jnp.where(lane_of(s.shape) < HEAD, s, 0.0)
        return jnp.concatenate([s, jnp.zeros((SPARE, LANES), jnp.float32)], axis=0)

    def diagonal(a, b):
        zero = jnp.zeros((LANES, LANES), jnp.float32)
        return split(jnp.concatenate([jnp.concatenate([a, zero], axis=1), jnp.concatenate([zero, b], axis=1)], axis=0))

    stores = []

    def store(i, p):
        for h in (2 * p, 2 * p + 1):
            copy = pltpu.make_async_copy(og.at[i, slot_rows(h)], outs[i].at[0, head_rows(h)], osems.at[i, h])
            copy.start()
            stores.append(copy)

    nn = ((1,), (0,))
    for p in range(heads // 2):
        rows = slice(p * PAIR, (p + 1) * PAIR)
        for h in (2 * p, 2 * p + 1):
            loads[0, h].wait()
            loads[1, h].wait()
        s = diagonal(state(0, 2 * p) * scale, state(0, 2 * p + 1) * scale)
        og[0, rows] = jnp.where(qb[rows] > 0, dot3(s, split(cb[rows]), nn), 0.0)
        store(0, p)
    for p in range(heads // 2):
        rows = slice(p * PAIR, (p + 1) * PAIR)
        for h in (2 * p, 2 * p + 1):
            loads[2, h].wait()
            loads[3, h].wait()
        a, b = state(1, 2 * p), state(1, 2 * p + 1)
        og[1, rows] = jnp.where(kb[rows] > 0, dot3(diagonal(a, b), split(vb[rows]), nn), 0.0)
        store(1, p)
        og[2, rows] = dot3(diagonal(a.T, b.T), split(jnp.maximum(kb[rows], 0.0)), nn)
        store(2, p)
    for copy in stores:
        copy.wait()


def gradients(scale, q, k, v, cot, own, other):
    _, width, spatial = q.shape
    heads = width // HEAD
    tiles = 4 * own[0].shape[0]
    smem = pl.BlockSpec(memory_space=pltpu.SMEM)
    hbm = pl.BlockSpec(memory_space=pl.ANY)
    array = pltpu.VMEM((heads * LANES, spatial), jnp.float32)
    return pl.pallas_call(
        functools.partial(grads_kernel, heads),
        out_shape=[jax.ShapeDtypeStruct(q.shape, jnp.float32)] * 3,
        in_specs=[smem, hbm, hbm, hbm, hbm] + [hbm] * 8,
        out_specs=[hbm] * 3,
        scratch_shapes=[
            array,
            array,
            array,
            array,
            pltpu.VMEM((2, tiles, 8, LANES), jnp.float32),
            pltpu.VMEM((3, heads * LANES, spatial), jnp.float32),
            pltpu.SemaphoreType.DMA((4, heads)),
            pltpu.SemaphoreType.DMA((2, 4)),
            pltpu.SemaphoreType.DMA((3, heads)),
        ],
        compiler_params=pltpu.CompilerParams(vmem_limit_bytes=20 << 20),
        name="grads",
    )(scale, q, k, v, cot, *own, *other)


def ring(n, k):
    return [(i, (i + k) % n) for i in range(n)]


def shards(queries, keys, values, cotangent):
    queries, keys, values, cotangent = (
        pltpu.with_memory_space_constraint(jnp.swapaxes(a, 1, 2), pltpu.HBM) for a in (queries, keys, values, cotangent)
    )
    _, width, spatial = queries.shape
    ny, nz, nx, nc = (lax.axis_size(a) for a in ("y", "z", "x", "c"))
    y, z, x, c = (lax.axis_index(a) for a in ("y", "z", "x", "c"))
    count = (y * nz + z + 1).astype(jnp.float32) * (spatial * nx * nc * HEAD)
    scale = (1.0 / jnp.sqrt(count)).reshape(1)
    step = nx * nz
    tiles = -(-(ROWS * (width // HEAD - 1)) // step) * step

    args = (scale, queries, keys, values, cotangent, tiles)
    sent = gram_state(0, *args)
    got = lax.ppermute(sent, "c", ring(nc, 1))
    both = gram_state(1, *args) + got

    n = tiles // nx
    piece = lambda k: lax.dynamic_slice_in_dim(both, lax.rem(x + k, nx) * n, n, 0)
    mine = piece(0)
    arrived = [lax.ppermute(piece(k), "x", ring(nx, k)) for k in (1, 3, 2)]
    mine = (mine + arrived[0]) + (arrived[1] + arrived[2])

    g = mine.reshape(nz, n // nz, 8, LANES)
    g = lax.all_to_all(g, "z", split_axis=0, concat_axis=0, tiled=True)
    total = g.sum(axis=0)
    carry = 0.0
    for k in range(1, ny):
        pairs = [(i * nc, (i + k) * nc) for i in range(ny - k)] + [((i + k) * nc + 1, i * nc + 1) for i in range(ny - k)]
        carry = carry + lax.ppermute(total, ("y", "c"), pairs)
    up, down = [], []
    run_up = run_down = carry
    for j in range(nz):
        run_up = run_up + g[j]
        up.append(run_up)
        run_down = run_down + g[nz - 1 - j]
        down.append(run_down)
    scanned = jnp.where(c == 0, jnp.stack(up), jnp.stack(down[::-1]))
    mine = lax.all_to_all(scanned, "z", split_axis=0, concat_axis=0, tiled=True)
    mine = mine.reshape(n, 8, LANES)

    own = [mine] + [lax.ppermute(mine, "x", ring(nx, k)) for k in range(1, nx)]
    other = [lax.ppermute(p, "c", ring(nc, 1)) for p in own]
    grads = gradients(scale, queries, keys, values, cotangent, own, other)
    return tuple(jnp.swapaxes(a, 1, 2) for a in grads)


def solution(mesh):
    torus = Mesh(mesh.devices.reshape(4, 8, 4, 2), ("y", "z", "x", "c"))
    spec = P(("y", "z"), ("x", "c"), None)
    return jax.shard_map(shards, mesh=torus, in_specs=(spec,) * 4, out_specs=(spec,) * 3, check_vma=False)
```

```python
import functools

import jax
import jax.numpy as jnp
from jax import lax
from jax.experimental import pallas as pl
from jax.experimental.pallas import tpu as pltpu
from jax.sharding import Mesh
from jax.sharding import PartitionSpec as P

HEAD = 112
LANES = 128
ROWS = HEAD // 8


def split(x):
    hi = x.astype(jnp.bfloat16)
    return hi, (x - hi.astype(jnp.float32)).astype(jnp.bfloat16)


def dot3(a, b, dims):
    (ah, al), (bh, bl) = a, b
    d = functools.partial(lax.dot_general, dimension_numbers=(dims, ((), ())), preferred_element_type=jnp.float32)
    rows = ah.shape[0]
    both = d(jnp.concatenate([ah, al], axis=0), bh)
    return both[:rows] + (both[rows:] + d(ah, bl))


SPLIT = 7
SPARE = LANES - HEAD
PAIR = 2 * LANES


def clear_pads(*refs):
    for ref in refs:
        heads, _, spatial = ref.shape
        ref[:, HEAD:] = jnp.zeros((heads, SPARE, spatial), jnp.float32)


def lane_of(shape):
    return lax.broadcasted_iota(jnp.int32, shape, 1)


def pair_of(ref, p):
    return ref[2 * p : 2 * p + 2].reshape(PAIR, ref.shape[2])


def gram_kernel(first, scale_ref, q_ref, k_ref, v_ref, c_ref, out_ref, left, right, sems):
    heads = left.shape[0]
    use_q = lax.axis_index("c") == first

    def copies(l_ref, r_ref):
        n = heads // 2
        return [
            pltpu.make_async_copy(src.at[pl.ds(i * n, n)], dst.at[pl.ds(i * n, n), pl.ds(0, HEAD)], sems.at[j, i])
            for i in range(2)
            for j, (src, dst) in enumerate(((l_ref, left), (r_ref, right)))
        ]

    @pl.when(use_q)
    def _():
        for copy in copies(q_ref, c_ref):
            copy.start()

    @pl.when(jnp.logical_not(use_q))
    def _():
        for copy in copies(k_ref, v_ref):
            copy.start()

    clear_pads(left, right)
    scale = jnp.where(use_q, scale_ref[0], 1.0)
    for copy in copies(k_ref, v_ref):
        copy.wait()
    for p in [SPLIT // 2] + [p for p in range(heads // 2) if p != SPLIT // 2]:
        gram = dot3(split(jnp.maximum(pair_of(left, p), 0.0)), split(pair_of(right, p)), ((1,), (1,))) * scale
        blocks = gram[:HEAD, :LANES], gram[LANES : LANES + HEAD, LANES:]
        if p == SPLIT // 2:
            shared = blocks[SPLIT % 2]
        for h, block in zip((2 * p, 2 * p + 1), blocks):
            if h == SPLIT:
                continue
            if h < SPLIT:
                part = pltpu.roll(shared, HEAD - h * SPARE, 1) if h * SPARE < HEAD else shared
                block = jnp.where(lane_of(block.shape) < HEAD, block, part)
            at = h if h < SPLIT else h - 1
            out_ref[at * ROWS : (at + 1) * ROWS] = block.reshape(ROWS, 8, LANES)
    used = (heads - 1) * ROWS
    out_ref[used:] = jnp.zeros((out_ref.shape[0] - used, 8, LANES), jnp.float32)


def gram_state(first, scale, q, k, v, cot, tiles):
    heads, _, spatial = q.shape
    smem = pl.BlockSpec(memory_space=pltpu.SMEM)
    hbm = pl.BlockSpec(memory_space=pl.ANY)
    slots = pltpu.VMEM((heads, LANES, spatial), jnp.float32)
    return pl.pallas_call(
        functools.partial(gram_kernel, first),
        out_shape=jax.ShapeDtypeStruct((tiles, 8, LANES), jnp.float32),
        in_specs=[smem, hbm, hbm, hbm, hbm],
        out_specs=pl.BlockSpec(memory_space=pltpu.VMEM),
        scratch_shapes=[slots, slots, pltpu.SemaphoreType.DMA((2, 2))],
        compiler_params=pltpu.CompilerParams(vmem_limit_bytes=16 << 20),
        cost_estimate=pl.CostEstimate(
            flops=6 * spatial * HEAD * HEAD * heads, bytes_accessed=8 * spatial * HEAD * heads, transcendentals=0
        ),
        name="gram",
    )(scale, q, k, v, cot)


def grads_kernel(scale_ref, q_ref, k_ref, v_ref, c_ref, *rest):
    own, other, outs, (qb, kb, vb, cb, st, wh, wl, og, sems, osems) = rest[:4], rest[4:8], rest[8:11], rest[11:]
    heads = qb.shape[0]
    loads = [
        pltpu.make_async_copy(src, dst.at[:, pl.ds(0, HEAD)], sems.at[i])
        for i, (src, dst) in enumerate(((c_ref, cb), (q_ref, qb), (v_ref, vb), (k_ref, kb)))
    ]
    for load in loads:
        load.start()
    x, core = lax.axis_index("x"), lax.axis_index("c")
    n = own[0].shape[0]
    for i, (a, b) in enumerate(zip(own, other)):
        at = pl.ds(lax.rem(x + 4 - i, 4) * n, n)
        st[core, at] = a[...]
        st[1 - core, at] = b[...]
    clear_pads(cb, vb, kb)
    scale = scale_ref[0]

    def state(kind, h):
        def block(at):
            return st[kind, at * ROWS : (at + 1) * ROWS].reshape(HEAD, LANES)

        if h == SPLIT:
            s = jnp.zeros((HEAD, LANES), jnp.float32)
            for i in range(SPLIT):
                lane = lane_of(s.shape)
                part = pltpu.roll(block(i), (i + 1) * SPARE, 1)
                s = jnp.where((lane >= i * SPARE) & (lane < (i + 1) * SPARE), part, s)
        else:
            s = block(h if h < SPLIT else h - 1)
            s = jnp.where(lane_of(s.shape) < HEAD, s, 0.0)
        return jnp.concatenate([s, jnp.zeros((SPARE, LANES), jnp.float32)], axis=0)

    zero = jnp.zeros((LANES, LANES), jnp.bfloat16)

    def put(kind, h, s):
        p, here = h // 2, h % 2
        for w, part in zip((wh, wl), split(s)):
            rows = slice(here * LANES, (here + 1) * LANES)
            w[kind, p, rows, here * LANES : (here + 1) * LANES] = part
            w[kind, p, rows, (1 - here) * LANES : (2 - here) * LANES] = zero

    for h in range(heads):
        put(0, h, state(0, h) * scale)
        s = state(1, h)
        put(1, h, s)
        put(2, h, s.T)

    def product(kind, p, d):
        return dot3((wh[kind, p], wl[kind, p]), split(d), ((1,), (0,)))

    def store(i, chunk):
        copy = pltpu.make_async_copy(og.at[i, chunk, pl.ds(0, HEAD)], outs[i].at[chunk], osems.at[i, chunk.start // 2])
        copy.start()
        stores.append(copy)

    stores = []
    loads[0].wait()
    loads[1].wait()
    pairs = heads // 2
    for p in range(pairs):
        out = jnp.where(pair_of(qb, p) > 0, product(0, p, pair_of(cb, p)), 0.0)
        og[0, 2 * p : 2 * p + 2] = out.reshape(2, LANES, out.shape[1])
    store(0, pl.ds(0, heads))
    loads[2].wait()
    loads[3].wait()
    for p in range(pairs):
        k = pair_of(kb, p)
        out = jnp.where(k > 0, product(1, p, pair_of(vb, p)), 0.0)
        og[1, 2 * p : 2 * p + 2] = out.reshape(2, LANES, out.shape[1])
        out = product(2, p, jnp.maximum(k, 0.0))
        og[2, 2 * p : 2 * p + 2] = out.reshape(2, LANES, out.shape[1])
        if p in (pairs // 2, pairs - 1):
            done = 0 if p == pairs // 2 else 2 * (pairs // 2) + 2
            chunk = pl.ds(done, 2 * p + 2 - done)
            store(1, chunk)
            store(2, chunk)
    for copy in stores:
        copy.wait()


def gradients(scale, q, k, v, cot, own, other):
    heads, _, spatial = q.shape
    tiles = 4 * own[0].shape[0]
    smem = pl.BlockSpec(memory_space=pltpu.SMEM)
    hbm = pl.BlockSpec(memory_space=pl.ANY)
    vmem = pl.BlockSpec(memory_space=pltpu.VMEM)
    own, other = ([pltpu.with_memory_space_constraint(a, pltpu.VMEM) for a in g] for g in (own, other))
    slots = pltpu.VMEM((heads, LANES, spatial), jnp.float32)
    weights = pltpu.VMEM((3, heads // 2, PAIR, PAIR), jnp.bfloat16)
    return pl.pallas_call(
        grads_kernel,
        out_shape=[jax.ShapeDtypeStruct(q.shape, jnp.float32)] * 3,
        in_specs=[smem, hbm, hbm, hbm, hbm] + [vmem] * 8,
        out_specs=[hbm] * 3,
        scratch_shapes=[
            slots,
            slots,
            slots,
            slots,
            pltpu.VMEM((2, tiles, 8, LANES), jnp.float32),
            weights,
            weights,
            pltpu.VMEM((3, heads, LANES, spatial), jnp.float32),
            pltpu.SemaphoreType.DMA((4,)),
            pltpu.SemaphoreType.DMA((3, heads // 2)),
        ],
        compiler_params=pltpu.CompilerParams(vmem_limit_bytes=24 << 20),
        name="grads",
    )(scale, q, k, v, cot, *own, *other)


def ring(n, k):
    return [(i, (i + k) % n) for i in range(n)]


def shards(queries, keys, values, cotangent):
    _, spatial, width = queries.shape
    heads = width // HEAD
    queries, keys, values, cotangent = (
        pltpu.with_memory_space_constraint(jnp.swapaxes(a, 1, 2).reshape(heads, HEAD, spatial), pltpu.HBM)
        for a in (queries, keys, values, cotangent)
    )
    ny, nz, nx, nc = (lax.axis_size(a) for a in ("y", "z", "x", "c"))
    y, z, x, c = (lax.axis_index(a) for a in ("y", "z", "x", "c"))
    count = (y * nz + z + 1).astype(jnp.float32) * (spatial * nx * nc * HEAD)
    scale = (1.0 / jnp.sqrt(count)).reshape(1)
    step = nx * nz
    tiles = -(-(ROWS * (heads - 1)) // step) * step

    args = (scale, queries, keys, values, cotangent, tiles)
    sent = gram_state(0, *args)
    got = lax.ppermute(sent, "c", ring(nc, 1))
    both = gram_state(1, *args) + got

    n = tiles // nx
    piece = lambda k: lax.dynamic_slice_in_dim(both, lax.rem(x + k, nx) * n, n, 0)
    mine = piece(0)
    arrived = [lax.ppermute(piece(k), "x", ring(nx, k)) for k in (1, 3, 2)]
    mine = (mine + arrived[0]) + (arrived[1] + arrived[2])

    g = mine.reshape(nz, n // nz, 8, LANES)
    g = lax.all_to_all(g, "z", split_axis=0, concat_axis=0, tiled=True)
    total = g.sum(axis=0)
    carry = 0.0
    for k in reversed(range(1, ny)):
        pairs = [(i * nc, (i + k) * nc) for i in range(ny - k)] + [((i + k) * nc + 1, i * nc + 1) for i in range(ny - k)]
        carry = carry + lax.ppermute(total, ("y", "c"), pairs)
    up, down = [], []
    run_up = run_down = carry
    for j in range(nz):
        run_up = run_up + g[j]
        up.append(run_up)
        run_down = run_down + g[nz - 1 - j]
        down.append(run_down)
    scanned = jnp.where(c == 0, jnp.stack(up), jnp.stack(down[::-1]))
    mine = lax.all_to_all(scanned, "z", split_axis=0, concat_axis=0, tiled=True)
    mine = mine.reshape(n, 8, LANES)

    own = [mine] + [lax.ppermute(mine, "x", ring(nx, k)) for k in range(1, nx)]
    other = [lax.ppermute(p, "c", ring(nc, 1)) for p in own]
    grads = gradients(scale, queries, keys, values, cotangent, own, other)
    return tuple(jnp.swapaxes(a.reshape(1, width, spatial), 1, 2) for a in grads)


def solution(mesh):
    torus = Mesh(mesh.devices.reshape(4, 8, 4, 2), ("y", "z", "x", "c"))
    spec = P(("y", "z"), ("x", "c"), None)
    return jax.shard_map(shards, mesh=torus, in_specs=(spec,) * 4, out_specs=(spec,) * 3, check_vma=False)
```

```python
import functools

import jax
import jax.numpy as jnp
from jax import lax
from jax.experimental import pallas as pl
from jax.experimental.pallas import tpu as pltpu
from jax.sharding import Mesh
from jax.sharding import PartitionSpec as P

HEAD = 112
LANES = 128
ROWS = HEAD // 8


def split(x):
    hi = x.astype(jnp.bfloat16)
    return hi, (x - hi.astype(jnp.float32)).astype(jnp.bfloat16)


def dot3(a, b, dims):
    (ah, al), (bh, bl) = a, b
    d = functools.partial(lax.dot_general, dimension_numbers=(dims, ((), ())), preferred_element_type=jnp.float32)
    rows = ah.shape[0]
    both = d(jnp.concatenate([ah, al], axis=0), bh)
    return both[:rows] + (both[rows:] + d(ah, bl))


SPLIT = 7
SPARE = LANES - HEAD
PAIR = 2 * LANES
HOPS = 0, 3, 1, 2


def clear_pads(*refs):
    for ref in refs:
        heads, _, spatial = ref.shape
        ref[:, HEAD:] = jnp.zeros((heads, SPARE, spatial), jnp.float32)


def lane_of(shape):
    return lax.broadcasted_iota(jnp.int32, shape, 1)


def pair_of(ref, p):
    return ref[2 * p : 2 * p + 2].reshape(PAIR, ref.shape[2])


def gram_kernel(first, scale_ref, q_ref, k_ref, v_ref, c_ref, out_ref, left, right, sems):
    heads = left.shape[0]
    use_q = lax.axis_index("c") == first

    def copies(l_ref, r_ref):
        n = heads // 2
        return [
            pltpu.make_async_copy(src.at[pl.ds(i * n, n)], dst.at[pl.ds(i * n, n), pl.ds(0, HEAD)], sems.at[j, i])
            for i in range(2)
            for j, (src, dst) in enumerate(((l_ref, left), (r_ref, right)))
        ]

    @pl.when(use_q)
    def _():
        for copy in copies(q_ref, c_ref):
            copy.start()

    @pl.when(jnp.logical_not(use_q))
    def _():
        for copy in copies(k_ref, v_ref):
            copy.start()

    clear_pads(left, right)
    scale = jnp.where(use_q, scale_ref[0], 1.0)
    for copy in copies(k_ref, v_ref):
        copy.wait()
    for p in [SPLIT // 2] + [p for p in range(heads // 2) if p != SPLIT // 2]:
        gram = dot3(split(jnp.maximum(pair_of(left, p), 0.0)), split(pair_of(right, p)), ((1,), (1,))) * scale
        blocks = gram[:HEAD, :LANES], gram[LANES : LANES + HEAD, LANES:]
        if p == SPLIT // 2:
            shared = blocks[SPLIT % 2]
        for h, block in zip((2 * p, 2 * p + 1), blocks):
            if h == SPLIT:
                continue
            if h < SPLIT:
                part = pltpu.roll(shared, HEAD - h * SPARE, 1) if h * SPARE < HEAD else shared
                block = jnp.where(lane_of(block.shape) < HEAD, block, part)
            at = h if h < SPLIT else h - 1
            out_ref[at * ROWS : (at + 1) * ROWS] = block.reshape(ROWS, 8, LANES)
    used = (heads - 1) * ROWS
    out_ref[used:] = jnp.zeros((out_ref.shape[0] - used, 8, LANES), jnp.float32)


def gram_state(first, scale, q, k, v, cot, tiles):
    heads, _, spatial = q.shape
    smem = pl.BlockSpec(memory_space=pltpu.SMEM)
    hbm = pl.BlockSpec(memory_space=pl.ANY)
    slots = pltpu.VMEM((heads, LANES, spatial), jnp.float32)
    return pl.pallas_call(
        functools.partial(gram_kernel, first),
        out_shape=jax.ShapeDtypeStruct((tiles, 8, LANES), jnp.float32),
        in_specs=[smem, hbm, hbm, hbm, hbm],
        out_specs=pl.BlockSpec(memory_space=pltpu.VMEM),
        scratch_shapes=[slots, slots, pltpu.SemaphoreType.DMA((2, 2))],
        compiler_params=pltpu.CompilerParams(vmem_limit_bytes=16 << 20),
        cost_estimate=pl.CostEstimate(
            flops=6 * spatial * HEAD * HEAD * heads, bytes_accessed=8 * spatial * HEAD * heads, transcendentals=0
        ),
        name="gram",
    )(scale, q, k, v, cot)


def grads_kernel(scale_ref, q_ref, k_ref, v_ref, c_ref, *rest):
    own, other, outs, (qb, kb, vb, cb, st, wh, wl, og, sems, osems) = rest[:4], rest[4:8], rest[8:11], rest[11:]
    heads = qb.shape[0]
    loads = [
        pltpu.make_async_copy(src, dst.at[:, pl.ds(0, HEAD)], sems.at[i])
        for i, (src, dst) in enumerate(((c_ref, cb), (q_ref, qb), (v_ref, vb), (k_ref, kb)))
    ]
    for load in loads:
        load.start()
    x, core = lax.axis_index("x"), lax.axis_index("c")
    n = own[0].shape[0]
    for hop, a, b in zip(HOPS, own, other):
        at = pl.ds(lax.rem(x + 4 - hop, 4) * n, n)
        st[core, at] = a[...]
        st[1 - core, at] = b[...]
    clear_pads(cb, vb, kb)
    scale = scale_ref[0]

    def state(kind, h):
        def block(at):
            return st[kind, at * ROWS : (at + 1) * ROWS].reshape(HEAD, LANES)

        if h == SPLIT:
            s = jnp.zeros((HEAD, LANES), jnp.float32)
            for i in range(SPLIT):
                lane = lane_of(s.shape)
                part = pltpu.roll(block(i), (i + 1) * SPARE, 1)
                s = jnp.where((lane >= i * SPARE) & (lane < (i + 1) * SPARE), part, s)
        else:
            s = block(h if h < SPLIT else h - 1)
            s = jnp.where(lane_of(s.shape) < HEAD, s, 0.0)
        return jnp.concatenate([s, jnp.zeros((SPARE, LANES), jnp.float32)], axis=0)

    zero = jnp.zeros((LANES, LANES), jnp.bfloat16)

    def put(kind, h, s):
        p, here = h // 2, h % 2
        for w, part in zip((wh, wl), split(s)):
            rows = slice(here * LANES, (here + 1) * LANES)
            w[kind, p, rows, here * LANES : (here + 1) * LANES] = part
            w[kind, p, rows, (1 - here) * LANES : (2 - here) * LANES] = zero

    for h in range(heads):
        put(0, h, state(0, h) * scale)
        s = state(1, h)
        put(1, h, s)
        put(2, h, s.T)

    def product(kind, p, d):
        return dot3((wh[kind, p], wl[kind, p]), split(d), ((1,), (0,)))

    def store(i, chunk):
        copy = pltpu.make_async_copy(og.at[i, chunk, pl.ds(0, HEAD)], outs[i].at[chunk], osems.at[i, chunk.start // 2])
        copy.start()
        stores.append(copy)

    stores = []
    loads[0].wait()
    loads[1].wait()
    pairs = heads // 2
    for p in range(pairs):
        out = jnp.where(pair_of(qb, p) > 0, product(0, p, pair_of(cb, p)), 0.0)
        og[0, 2 * p : 2 * p + 2] = out.reshape(2, LANES, out.shape[1])
    store(0, pl.ds(0, heads))
    loads[2].wait()
    loads[3].wait()
    for p in range(pairs):
        k = pair_of(kb, p)
        out = jnp.where(k > 0, product(1, p, pair_of(vb, p)), 0.0)
        og[1, 2 * p : 2 * p + 2] = out.reshape(2, LANES, out.shape[1])
        out = product(2, p, jnp.maximum(k, 0.0))
        og[2, 2 * p : 2 * p + 2] = out.reshape(2, LANES, out.shape[1])
        if p in (pairs // 2, pairs - 1):
            done = 0 if p == pairs // 2 else 2 * (pairs // 2) + 2
            chunk = pl.ds(done, 2 * p + 2 - done)
            store(1, chunk)
            store(2, chunk)
    for copy in stores:
        copy.wait()


def gradients(scale, q, k, v, cot, own, other):
    heads, _, spatial = q.shape
    tiles = 4 * own[0].shape[0]
    smem = pl.BlockSpec(memory_space=pltpu.SMEM)
    hbm = pl.BlockSpec(memory_space=pl.ANY)
    vmem = pl.BlockSpec(memory_space=pltpu.VMEM)
    own, other = ([pltpu.with_memory_space_constraint(a, pltpu.VMEM) for a in g] for g in (own, other))
    slots = pltpu.VMEM((heads, LANES, spatial), jnp.float32)
    weights = pltpu.VMEM((3, heads // 2, PAIR, PAIR), jnp.bfloat16)
    return pl.pallas_call(
        grads_kernel,
        out_shape=[jax.ShapeDtypeStruct(q.shape, jnp.float32)] * 3,
        in_specs=[smem, hbm, hbm, hbm, hbm] + [vmem] * 8,
        out_specs=[hbm] * 3,
        scratch_shapes=[
            slots,
            slots,
            slots,
            slots,
            pltpu.VMEM((2, tiles, 8, LANES), jnp.float32),
            weights,
            weights,
            pltpu.VMEM((3, heads, LANES, spatial), jnp.float32),
            pltpu.SemaphoreType.DMA((4,)),
            pltpu.SemaphoreType.DMA((3, heads // 2)),
        ],
        compiler_params=pltpu.CompilerParams(vmem_limit_bytes=24 << 20),
        name="grads",
    )(scale, q, k, v, cot, *own, *other)


def ring(n, k):
    return [(i, (i + k) % n) for i in range(n)]


def shards(queries, keys, values, cotangent):
    _, spatial, width = queries.shape
    heads = width // HEAD
    queries, keys, values, cotangent = (
        pltpu.with_memory_space_constraint(jnp.swapaxes(a, 1, 2).reshape(heads, HEAD, spatial), pltpu.HBM)
        for a in (queries, keys, values, cotangent)
    )
    ny, nz, nx, nc = (lax.axis_size(a) for a in ("y", "z", "x", "c"))
    y, z, x, c = (lax.axis_index(a) for a in ("y", "z", "x", "c"))
    count = (y * nz + z + 1).astype(jnp.float32) * (spatial * nx * nc * HEAD)
    scale = (1.0 / jnp.sqrt(count)).reshape(1)
    step = nx * nz
    tiles = -(-(ROWS * (heads - 1)) // step) * step

    args = (scale, queries, keys, values, cotangent, tiles)
    sent = gram_state(0, *args)
    got = lax.ppermute(sent, "c", ring(nc, 1))
    both = gram_state(1, *args) + got

    n = tiles // nx
    piece = lambda k: lax.dynamic_slice_in_dim(both, lax.rem(x + k, nx) * n, n, 0)
    mine = piece(0)
    arrived = [lax.ppermute(piece(k), "x", ring(nx, k)) for k in (1, 3, 2)]
    mine = (mine + arrived[0]) + (arrived[1] + arrived[2])

    g = mine.reshape(nz, n // nz, 8, LANES)
    g = lax.all_to_all(g, "z", split_axis=0, concat_axis=0, tiled=True)
    total = g.sum(axis=0)
    def over_y(value, *hops):
        pairs = [(i * nc, j * nc) for i, j in hops] + [((ny - 1 - i) * nc + 1, (ny - 1 - j) * nc + 1) for i, j in hops]
        return lax.ppermute(value, ("y", "c"), pairs)

    carry = over_y(total, (0, 1), (2, 3))
    both = total + carry
    carry = carry + (over_y(both, (1, 2)) + over_y(both, (1, 3)))
    up, down = [], []
    run_up = run_down = carry
    for j in range(nz):
        run_up = run_up + g[j]
        up.append(run_up)
        run_down = run_down + g[nz - 1 - j]
        down.append(run_down)
    scanned = jnp.where(c == 0, jnp.stack(up), jnp.stack(down[::-1]))
    mine = lax.all_to_all(scanned, "z", split_axis=0, concat_axis=0, tiled=True)
    mine = mine.reshape(n, 8, LANES)

    own = [mine] + [lax.ppermute(mine, "x", ring(nx, k)) for k in HOPS[1:]]
    other = [lax.ppermute(p, "c", ring(nc, 1)) for p in own]
    grads = gradients(scale, queries, keys, values, cotangent, own, other)
    return tuple(jnp.swapaxes(a.reshape(1, width, spatial), 1, 2) for a in grads)


def solution(mesh):
    torus = Mesh(mesh.devices.reshape(4, 8, 4, 2), ("y", "z", "x", "c"))
    spec = P(("y", "z"), ("x", "c"), None)
    return jax.shard_map(shards, mesh=torus, in_specs=(spec,) * 4, out_specs=(spec,) * 3, check_vma=False)
```

```python
import functools

import jax
import jax.numpy as jnp
from jax import lax
from jax.experimental import pallas as pl
from jax.experimental.pallas import tpu as pltpu
from jax.sharding import Mesh
from jax.sharding import PartitionSpec as P

HEAD = 112
LANES = 128
ROWS = HEAD // 8


def split(x):
    hi = x.astype(jnp.bfloat16)
    return hi, (x - hi.astype(jnp.float32)).astype(jnp.bfloat16)


def dot3(a, b, dims):
    (ah, al), (bh, bl) = a, b
    d = functools.partial(lax.dot_general, dimension_numbers=(dims, ((), ())), preferred_element_type=jnp.float32)
    rows = ah.shape[0]
    both = d(jnp.concatenate([ah, al], axis=0), bh)
    return both[:rows] + (both[rows:] + d(ah, bl))


SPLIT = 7
SPARE = LANES - HEAD
PAIR = 2 * LANES
HOPS = 0, 3, 1, 2


def clear_pads(*refs):
    for ref in refs:
        heads, _, spatial = ref.shape
        ref[:, HEAD:] = jnp.zeros((heads, SPARE, spatial), jnp.float32)


def lane_of(shape):
    return lax.broadcasted_iota(jnp.int32, shape, 1)


def pair_of(ref, p):
    return ref[2 * p : 2 * p + 2].reshape(PAIR, ref.shape[2])


def gram_kernel(first, scale_ref, q_ref, k_ref, v_ref, c_ref, out_ref, left, right, sems):
    heads = left.shape[0]
    use_q = lax.axis_index("c") == first

    def copies(l_ref, r_ref):
        n = heads // 2
        return [
            pltpu.make_async_copy(src.at[pl.ds(i * n, n)], dst.at[pl.ds(i * n, n), pl.ds(0, HEAD)], sems.at[j, i])
            for i in range(2)
            for j, (src, dst) in enumerate(((l_ref, left), (r_ref, right)))
        ]

    @pl.when(use_q)
    def _():
        for copy in copies(q_ref, c_ref):
            copy.start()

    @pl.when(jnp.logical_not(use_q))
    def _():
        for copy in copies(k_ref, v_ref):
            copy.start()

    clear_pads(left, right)
    scale = jnp.where(use_q, scale_ref[0], 1.0)
    for copy in copies(k_ref, v_ref):
        copy.wait()
    for p in [SPLIT // 2] + [p for p in range(heads // 2) if p != SPLIT // 2]:
        gram = dot3(split(jnp.maximum(pair_of(left, p), 0.0)), split(pair_of(right, p)), ((1,), (1,))) * scale
        blocks = gram[:HEAD, :LANES], gram[LANES : LANES + HEAD, LANES:]
        if p == SPLIT // 2:
            shared = blocks[SPLIT % 2]
        for h, block in zip((2 * p, 2 * p + 1), blocks):
            if h == SPLIT:
                continue
            if h < SPLIT:
                part = pltpu.roll(shared, HEAD - h * SPARE, 1) if h * SPARE < HEAD else shared
                block = jnp.where(lane_of(block.shape) < HEAD, block, part)
            at = h if h < SPLIT else h - 1
            out_ref[at * ROWS : (at + 1) * ROWS] = block.reshape(ROWS, 8, LANES)
    used = (heads - 1) * ROWS
    out_ref[used:] = jnp.zeros((out_ref.shape[0] - used, 8, LANES), jnp.float32)


def gram_state(first, scale, q, k, v, cot, tiles):
    heads, _, spatial = q.shape
    smem = pl.BlockSpec(memory_space=pltpu.SMEM)
    hbm = pl.BlockSpec(memory_space=pl.ANY)
    slots = pltpu.VMEM((heads, LANES, spatial), jnp.float32)
    return pl.pallas_call(
        functools.partial(gram_kernel, first),
        out_shape=jax.ShapeDtypeStruct((tiles, 8, LANES), jnp.float32),
        in_specs=[smem, hbm, hbm, hbm, hbm],
        out_specs=pl.BlockSpec(memory_space=pltpu.VMEM),
        scratch_shapes=[slots, slots, pltpu.SemaphoreType.DMA((2, 2))],
        compiler_params=pltpu.CompilerParams(vmem_limit_bytes=16 << 20),
        cost_estimate=pl.CostEstimate(
            flops=6 * spatial * HEAD * HEAD * heads, bytes_accessed=8 * spatial * HEAD * heads, transcendentals=0
        ),
        name="gram",
    )(scale, q, k, v, cot)


def grads_kernel(scale_ref, q_ref, k_ref, v_ref, c_ref, *rest):
    own, other, outs, (qb, kb, vb, cb, st, wh, wl, og, sems, osems) = rest[:4], rest[4:8], rest[8:11], rest[11:]
    heads = qb.shape[0]
    loads = [
        pltpu.make_async_copy(src, dst.at[:, pl.ds(0, HEAD)], sems.at[i])
        for i, (src, dst) in enumerate(((c_ref, cb), (q_ref, qb), (v_ref, vb), (k_ref, kb)))
    ]
    for load in loads:
        load.start()
    x, core = lax.axis_index("x"), lax.axis_index("c")
    n = own[0].shape[0]
    for hop, a, b in zip(HOPS, own, other):
        at = pl.ds(lax.rem(x + 4 - hop, 4) * n, n)
        st[core, at] = a[...]
        st[1 - core, at] = b[...]
    clear_pads(cb, vb, kb)
    scale = scale_ref[0]

    def state(kind, h):
        def block(at):
            return st[kind, at * ROWS : (at + 1) * ROWS].reshape(HEAD, LANES)

        if h == SPLIT:
            s = jnp.zeros((HEAD, LANES), jnp.float32)
            for i in range(SPLIT):
                lane = lane_of(s.shape)
                part = pltpu.roll(block(i), (i + 1) * SPARE, 1)
                s = jnp.where((lane >= i * SPARE) & (lane < (i + 1) * SPARE), part, s)
        else:
            s = block(h if h < SPLIT else h - 1)
            s = jnp.where(lane_of(s.shape) < HEAD, s, 0.0)
        return jnp.concatenate([s, jnp.zeros((SPARE, LANES), jnp.float32)], axis=0)

    zero = jnp.zeros((LANES, LANES), jnp.bfloat16)

    def put(kind, h, s):
        p, here = h // 2, h % 2
        for w, part in zip((wh, wl), split(s)):
            rows = slice(here * LANES, (here + 1) * LANES)
            w[kind, p, rows, here * LANES : (here + 1) * LANES] = part
            w[kind, p, rows, (1 - here) * LANES : (2 - here) * LANES] = zero

    for h in range(heads):
        put(0, h, state(0, h) * scale)
        s = state(1, h)
        put(1, h, s)
        put(2, h, s.T)

    def product(kind, p, d):
        return dot3((wh[kind, p], wl[kind, p]), split(d), ((1,), (0,)))

    def store(i, chunk):
        copy = pltpu.make_async_copy(og.at[i, chunk, pl.ds(0, HEAD)], outs[i].at[chunk], osems.at[i, chunk.start // 2])
        copy.start()
        stores.append(copy)

    stores = []
    loads[0].wait()
    loads[1].wait()
    pairs = heads // 2
    for p in range(pairs):
        out = jnp.where(pair_of(qb, p) > 0, product(0, p, pair_of(cb, p)), 0.0)
        og[0, 2 * p : 2 * p + 2] = out.reshape(2, LANES, out.shape[1])
    store(0, pl.ds(0, heads))
    loads[2].wait()
    loads[3].wait()
    for p in range(pairs):
        k = pair_of(kb, p)
        out = jnp.where(k > 0, product(1, p, pair_of(vb, p)), 0.0)
        og[1, 2 * p : 2 * p + 2] = out.reshape(2, LANES, out.shape[1])
        out = product(2, p, jnp.maximum(k, 0.0))
        og[2, 2 * p : 2 * p + 2] = out.reshape(2, LANES, out.shape[1])
        if p in (pairs // 2, pairs - 1):
            done = 0 if p == pairs // 2 else 2 * (pairs // 2) + 2
            chunk = pl.ds(done, 2 * p + 2 - done)
            store(1, chunk)
            store(2, chunk)
    for copy in stores:
        copy.wait()


def gradients(scale, q, k, v, cot, own, other):
    heads, _, spatial = q.shape
    tiles = 4 * own[0].shape[0]
    smem = pl.BlockSpec(memory_space=pltpu.SMEM)
    hbm = pl.BlockSpec(memory_space=pl.ANY)
    vmem = pl.BlockSpec(memory_space=pltpu.VMEM)
    own, other = ([pltpu.with_memory_space_constraint(a, pltpu.VMEM) for a in g] for g in (own, other))
    slots = pltpu.VMEM((heads, LANES, spatial), jnp.float32)
    weights = pltpu.VMEM((3, heads // 2, PAIR, PAIR), jnp.bfloat16)
    return pl.pallas_call(
        grads_kernel,
        out_shape=[jax.ShapeDtypeStruct(q.shape, jnp.float32)] * 3,
        in_specs=[smem, hbm, hbm, hbm, hbm] + [vmem] * 8,
        out_specs=[hbm] * 3,
        scratch_shapes=[
            slots,
            slots,
            slots,
            slots,
            pltpu.VMEM((2, tiles, 8, LANES), jnp.float32),
            weights,
            weights,
            pltpu.VMEM((3, heads, LANES, spatial), jnp.float32),
            pltpu.SemaphoreType.DMA((4,)),
            pltpu.SemaphoreType.DMA((3, heads // 2)),
        ],
        compiler_params=pltpu.CompilerParams(vmem_limit_bytes=24 << 20),
        name="grads",
    )(scale, q, k, v, cot, *own, *other)


def ring(n, k):
    return [(i, (i + k) % n) for i in range(n)]


def shards(queries, keys, values, cotangent):
    _, spatial, width = queries.shape
    heads = width // HEAD
    queries, keys, values, cotangent = (
        pltpu.with_memory_space_constraint(jnp.swapaxes(a, 1, 2).reshape(heads, HEAD, spatial), pltpu.HBM)
        for a in (queries, keys, values, cotangent)
    )
    ny, nz, nx, nc = (lax.axis_size(a) for a in ("y", "z", "x", "c"))
    y, z, x, c = (lax.axis_index(a) for a in ("y", "z", "x", "c"))
    count = (y * nz + z + 1).astype(jnp.float32) * (spatial * nx * nc * HEAD)
    scale = (1.0 / jnp.sqrt(count)).reshape(1)
    step = nx * nz
    tiles = -(-(ROWS * (heads - 1)) // step) * step

    args = (scale, queries, keys, values, cotangent, tiles)
    sent = gram_state(0, *args)
    got = lax.ppermute(sent, "c", ring(nc, 1))
    both = gram_state(1, *args) + got

    n = tiles // nx
    piece = lambda k: lax.dynamic_slice_in_dim(both, lax.rem(x + k, nx) * n, n, 0)
    mine = piece(0)
    arrived = [lax.ppermute(piece(k), "x", ring(nx, k)) for k in (1, 3, 2)]
    mine = (mine + arrived[0]) + (arrived[1] + arrived[2])

    g = mine.reshape(nz, n // nz, 8, LANES)
    g = lax.all_to_all(g, "z", split_axis=0, concat_axis=0, tiled=True)
    total = g.sum(axis=0)
    totals = lax.all_to_all(jnp.broadcast_to(total, (ny, *total.shape)), "y", split_axis=0, concat_axis=0, tiled=True)
    order = jnp.arange(ny, dtype=jnp.int32).reshape(ny, 1, 1, 1)
    earlier = jnp.where(c == 0, order < y, order > y)
    carry = jnp.where(earlier, totals, 0.0).sum(axis=0)
    up, down = [], []
    run_up = run_down = carry
    for j in range(nz):
        run_up = run_up + g[j]
        up.append(run_up)
        run_down = run_down + g[nz - 1 - j]
        down.append(run_down)
    scanned = jnp.where(c == 0, jnp.stack(up), jnp.stack(down[::-1]))
    mine = lax.all_to_all(scanned, "z", split_axis=0, concat_axis=0, tiled=True)
    mine = mine.reshape(n, 8, LANES)

    own = [mine] + [lax.ppermute(mine, "x", ring(nx, k)) for k in HOPS[1:]]
    other = [lax.ppermute(p, "c", ring(nc, 1)) for p in own]
    grads = gradients(scale, queries, keys, values, cotangent, own, other)
    return tuple(jnp.swapaxes(a.reshape(1, width, spatial), 1, 2) for a in grads)


def solution(mesh):
    torus = Mesh(mesh.devices.reshape(4, 8, 4, 2), ("y", "z", "x", "c"))
    spec = P(("y", "z"), ("x", "c"), None)
    return jax.shard_map(shards, mesh=torus, in_specs=(spec,) * 4, out_specs=(spec,) * 3, check_vma=False)
```

```python
import functools

import jax
import jax.numpy as jnp
from jax import lax
from jax.experimental import pallas as pl
from jax.experimental.pallas import tpu as pltpu
from jax.sharding import Mesh
from jax.sharding import PartitionSpec as P

HEAD = 112
LANES = 128
ROWS = HEAD // 8


def split(x):
    hi = x.astype(jnp.bfloat16)
    return hi, (x - hi.astype(jnp.float32)).astype(jnp.bfloat16)


def dot3(a, b, dims):
    (ah, al), (bh, bl) = a, b
    d = functools.partial(lax.dot_general, dimension_numbers=(dims, ((), ())), preferred_element_type=jnp.float32)
    rows = ah.shape[0]
    both = d(jnp.concatenate([ah, al], axis=0), bh)
    return both[:rows] + (both[rows:] + d(ah, bl))


SPLIT = 7
SPARE = LANES - HEAD
PAIR = 2 * LANES
HOPS = 0, 3, 1, 2


def clear_pads(*refs):
    for ref in refs:
        heads, _, spatial = ref.shape
        ref[:, HEAD:] = jnp.zeros((heads, SPARE, spatial), jnp.float32)


def lane_of(shape):
    return lax.broadcasted_iota(jnp.int32, shape, 1)


def pair_of(ref, p):
    return ref[2 * p : 2 * p + 2].reshape(PAIR, ref.shape[2])


def gram_kernel(first, scale_ref, q_ref, k_ref, v_ref, c_ref, out_ref, left, right, sems):
    heads = left.shape[0]
    use_q = lax.axis_index("c") == first

    def copies(l_ref, r_ref):
        n = heads // 2
        return [
            pltpu.make_async_copy(src.at[pl.ds(i * n, n)], dst.at[pl.ds(i * n, n), pl.ds(0, HEAD)], sems.at[j, i])
            for i in range(2)
            for j, (src, dst) in enumerate(((l_ref, left), (r_ref, right)))
        ]

    @pl.when(use_q)
    def _():
        for copy in copies(q_ref, c_ref):
            copy.start()

    @pl.when(jnp.logical_not(use_q))
    def _():
        for copy in copies(k_ref, v_ref):
            copy.start()

    clear_pads(left, right)
    scale = jnp.where(use_q, scale_ref[0], 1.0)
    for copy in copies(k_ref, v_ref):
        copy.wait()
    for p in [SPLIT // 2] + [p for p in range(heads // 2) if p != SPLIT // 2]:
        gram = dot3(split(jnp.maximum(pair_of(left, p), 0.0)), split(pair_of(right, p)), ((1,), (1,))) * scale
        blocks = gram[:HEAD, :LANES], gram[LANES : LANES + HEAD, LANES:]
        if p == SPLIT // 2:
            shared = blocks[SPLIT % 2]
        for h, block in zip((2 * p, 2 * p + 1), blocks):
            if h == SPLIT:
                continue
            if h < SPLIT:
                part = pltpu.roll(shared, HEAD - h * SPARE, 1) if h * SPARE < HEAD else shared
                block = jnp.where(lane_of(block.shape) < HEAD, block, part)
            at = h if h < SPLIT else h - 1
            out_ref[at * ROWS : (at + 1) * ROWS] = block.reshape(ROWS, 8, LANES)
    used = (heads - 1) * ROWS
    out_ref[used:] = jnp.zeros((out_ref.shape[0] - used, 8, LANES), jnp.float32)


def gram_state(first, scale, q, k, v, cot, tiles):
    heads, _, spatial = q.shape
    smem = pl.BlockSpec(memory_space=pltpu.SMEM)
    hbm = pl.BlockSpec(memory_space=pl.ANY)
    slots = pltpu.VMEM((heads, LANES, spatial), jnp.float32)
    return pl.pallas_call(
        functools.partial(gram_kernel, first),
        out_shape=jax.ShapeDtypeStruct((tiles, 8, LANES), jnp.float32),
        in_specs=[smem, hbm, hbm, hbm, hbm],
        out_specs=pl.BlockSpec(memory_space=pltpu.VMEM),
        scratch_shapes=[slots, slots, pltpu.SemaphoreType.DMA((2, 2))],
        compiler_params=pltpu.CompilerParams(vmem_limit_bytes=16 << 20),
        cost_estimate=pl.CostEstimate(
            flops=6 * spatial * HEAD * HEAD * heads, bytes_accessed=8 * spatial * HEAD * heads, transcendentals=0
        ),
        name="gram",
    )(scale, q, k, v, cot)


def grads_kernel(scale_ref, q_ref, k_ref, v_ref, c_ref, *rest):
    own, other, outs, (qb, kb, vb, cb, st, wh, wl, og, sems, osems) = rest[:4], rest[4:8], rest[8:11], rest[11:]
    heads = qb.shape[0]
    loads = [
        pltpu.make_async_copy(src, dst.at[:, pl.ds(0, HEAD)], sems.at[i])
        for i, (src, dst) in enumerate(((c_ref, cb), (q_ref, qb), (v_ref, vb), (k_ref, kb)))
    ]
    for load in loads:
        load.start()
    x, core = lax.axis_index("x"), lax.axis_index("c")
    n = own[0].shape[0]
    for hop, a, b in zip(HOPS, own, other):
        at = pl.ds(lax.rem(x + 4 - hop, 4) * n, n)
        st[core, at] = a[...]
        st[1 - core, at] = b[...]
    clear_pads(cb, vb, kb)
    scale = scale_ref[0]

    def state(kind, h):
        def block(at):
            return st[kind, at * ROWS : (at + 1) * ROWS].reshape(HEAD, LANES)

        if h == SPLIT:
            s = jnp.zeros((HEAD, LANES), jnp.float32)
            for i in range(SPLIT):
                lane = lane_of(s.shape)
                part = pltpu.roll(block(i), (i + 1) * SPARE, 1)
                s = jnp.where((lane >= i * SPARE) & (lane < (i + 1) * SPARE), part, s)
        else:
            s = block(h if h < SPLIT else h - 1)
            s = jnp.where(lane_of(s.shape) < HEAD, s, 0.0)
        return jnp.concatenate([s, jnp.zeros((SPARE, LANES), jnp.float32)], axis=0)

    zero = jnp.zeros((LANES, LANES), jnp.bfloat16)

    def put(kind, h, s):
        p, here = h // 2, h % 2
        for w, part in zip((wh, wl), split(s)):
            rows = slice(here * LANES, (here + 1) * LANES)
            w[kind, p, rows, here * LANES : (here + 1) * LANES] = part
            w[kind, p, rows, (1 - here) * LANES : (2 - here) * LANES] = zero

    for h in range(heads):
        put(0, h, state(0, h) * scale)
        s = state(1, h)
        put(1, h, s)
        put(2, h, s.T)

    def product(kind, p, d):
        return dot3((wh[kind, p], wl[kind, p]), split(d), ((1,), (0,)))

    def store(i, chunk):
        copy = pltpu.make_async_copy(og.at[i, chunk, pl.ds(0, HEAD)], outs[i].at[chunk], osems.at[i, chunk.start // 2])
        copy.start()
        stores.append(copy)

    stores = []
    loads[0].wait()
    loads[1].wait()
    pairs = heads // 2
    for p in range(pairs):
        out = jnp.where(pair_of(qb, p) > 0, product(0, p, pair_of(cb, p)), 0.0)
        og[0, 2 * p : 2 * p + 2] = out.reshape(2, LANES, out.shape[1])
    store(0, pl.ds(0, heads))
    loads[2].wait()
    loads[3].wait()
    for p in range(pairs):
        k = pair_of(kb, p)
        out = jnp.where(k > 0, product(1, p, pair_of(vb, p)), 0.0)
        og[1, 2 * p : 2 * p + 2] = out.reshape(2, LANES, out.shape[1])
        out = product(2, p, jnp.maximum(k, 0.0))
        og[2, 2 * p : 2 * p + 2] = out.reshape(2, LANES, out.shape[1])
        if p in (pairs // 2, pairs - 1):
            done = 0 if p == pairs // 2 else 2 * (pairs // 2) + 2
            chunk = pl.ds(done, 2 * p + 2 - done)
            store(1, chunk)
            store(2, chunk)
    for copy in stores:
        copy.wait()


def gradients(scale, q, k, v, cot, own, other):
    heads, _, spatial = q.shape
    tiles = 4 * own[0].shape[0]
    smem = pl.BlockSpec(memory_space=pltpu.SMEM)
    hbm = pl.BlockSpec(memory_space=pl.ANY)
    vmem = pl.BlockSpec(memory_space=pltpu.VMEM)
    own, other = ([pltpu.with_memory_space_constraint(a, pltpu.VMEM) for a in g] for g in (own, other))
    slots = pltpu.VMEM((heads, LANES, spatial), jnp.float32)
    weights = pltpu.VMEM((3, heads // 2, PAIR, PAIR), jnp.bfloat16)
    return pl.pallas_call(
        grads_kernel,
        out_shape=[jax.ShapeDtypeStruct(q.shape, jnp.float32)] * 3,
        in_specs=[smem, hbm, hbm, hbm, hbm] + [vmem] * 8,
        out_specs=[hbm] * 3,
        scratch_shapes=[
            slots,
            slots,
            slots,
            slots,
            pltpu.VMEM((2, tiles, 8, LANES), jnp.float32),
            weights,
            weights,
            pltpu.VMEM((3, heads, LANES, spatial), jnp.float32),
            pltpu.SemaphoreType.DMA((4,)),
            pltpu.SemaphoreType.DMA((3, heads // 2)),
        ],
        compiler_params=pltpu.CompilerParams(vmem_limit_bytes=24 << 20),
        name="grads",
    )(scale, q, k, v, cot, *own, *other)


def scan_kernel(g_ref, out_ref):
    frames = g_ref.shape[0]
    up = lax.axis_index("c") == 0
    run = jnp.zeros(g_ref.shape[1:], jnp.float32)
    for i in range(frames):
        at = jnp.where(up, i, frames - 1 - i)
        run = run + g_ref[at]
        out_ref[at] = run


def scanned(g):
    vmem = pl.BlockSpec(memory_space=pltpu.VMEM)
    return pl.pallas_call(
        scan_kernel,
        out_shape=pltpu.VMEM(g.shape, jnp.float32),
        in_specs=[vmem],
        out_specs=vmem,
        compiler_params=pltpu.CompilerParams(vmem_limit_bytes=4 << 20),
        name="scan",
    )(pltpu.with_memory_space_constraint(g, pltpu.VMEM))


def ring(n, k):
    return [(i, (i + k) % n) for i in range(n)]


def shards(queries, keys, values, cotangent):
    _, spatial, width = queries.shape
    heads = width // HEAD
    queries, keys, values, cotangent = (
        pltpu.with_memory_space_constraint(jnp.swapaxes(a, 1, 2).reshape(heads, HEAD, spatial), pltpu.HBM)
        for a in (queries, keys, values, cotangent)
    )
    ny, nz, nx, nc = (lax.axis_size(a) for a in ("y", "z", "x", "c"))
    y, z, x, c = (lax.axis_index(a) for a in ("y", "z", "x", "c"))
    count = (y * nz + z + 1).astype(jnp.float32) * (spatial * nx * nc * HEAD)
    scale = (1.0 / jnp.sqrt(count)).reshape(1)
    step = nx * ny * nz
    tiles = -(-(ROWS * (heads - 1)) // step) * step

    args = (scale, queries, keys, values, cotangent, tiles)
    sent = gram_state(0, *args)
    got = lax.ppermute(sent, "c", ring(nc, 1))
    both = gram_state(1, *args) + got

    n = tiles // nx
    piece = lambda k: lax.dynamic_slice_in_dim(both, lax.rem(x + k, nx) * n, n, 0)
    mine = piece(0)
    arrived = [lax.ppermute(piece(k), "x", ring(nx, k)) for k in (1, 3, 2)]
    mine = (mine + arrived[0]) + (arrived[1] + arrived[2])

    frames = ny * nz
    g = mine.reshape(frames, n // frames * 8, LANES)
    g = lax.all_to_all(g, ("y", "z"), split_axis=0, concat_axis=0, tiled=True)
    mine = lax.all_to_all(scanned(g), ("y", "z"), split_axis=0, concat_axis=0, tiled=True)
    mine = mine.reshape(n, 8, LANES)

    own = [mine] + [lax.ppermute(mine, "x", ring(nx, k)) for k in HOPS[1:]]
    other = [lax.ppermute(p, "c", ring(nc, 1)) for p in own]
    grads = gradients(scale, queries, keys, values, cotangent, own, other)
    return tuple(jnp.swapaxes(a.reshape(1, width, spatial), 1, 2) for a in grads)


def solution(mesh):
    torus = Mesh(mesh.devices.reshape(4, 8, 4, 2), ("y", "z", "x", "c"))
    spec = P(("y", "z"), ("x", "c"), None)
    return jax.shard_map(shards, mesh=torus, in_specs=(spec,) * 4, out_specs=(spec,) * 3, check_vma=False)
```
